512 devices in a mesh: dp: 4 (over y_lo), head: 8 (over z), ctx: 16 (over x, y_hi, core).
Axes of the slice: x: 4, y: 8 (y_hi: 2, y_lo: 4; y = y_hi * 4 + y_lo), z: 8, core: 2. Of those that a mesh axis runs over, the one named last changes fastest.
Arguments:
- query_rows: bfloat16 [16384, 8192], P(('dp', 'ctx'), 'head'), parts along dimension 0, may hold values from -12 to 12
- key_rows: bfloat16 [16384, 1024], P(('dp', 'ctx'), 'head'), parts along dimension 0, may hold values from -4 to 4
- stored_value_rows: bfloat16 [16384, 1024], P(('dp', 'ctx'), 'head'), parts along dimension 0, may hold values from -6 to 6
- out_grad: bfloat16 [16384, 8192], P(('dp', 'ctx'), 'head'), parts along dimension 0, may hold values from -6 to 6
- block_table: int32 [64, 2], P('dp'), parts along dimension 0, may hold values from 0 to 31, as said below
- pattern: int32 [128, 10], P('dp'), parts along dimension 0, may hold values from 0 to 31, as said below
Outputs:
- attended: bfloat16 [16384, 8192], P(('dp', 'ctx'), 'head'), parts along dimension 0
- query_grad: bfloat16 [16384, 8192], P(('dp', 'ctx'), 'head'), parts along dimension 0
- key_grad: bfloat16 [16384, 1024], P(('dp', 'ctx'), 'head'), parts along dimension 0
- value_grad: bfloat16 [16384, 1024], P(('dp', 'ctx'), 'head'), parts along dimension 0
The draws below stay inside these ranges and needn't reach their ends.
There are 4 independent parts, one for each index of `dp`. The reference program is written for one: setup_inputs(seed, part) draws one part's arguments, and reference() takes and returns one part's arrays. A program takes and returns all parts, laid end to end along the dimension named above; each array names one. Nothing has to cross between parts.
Inputs may be any that keep to these rules, and one draw needn't show every extreme that they name: `pattern`: row b lists the key blocks that sequence block b reads, in no order; every entry is at most b; b, max(b - 1, 0) and 0 are always listed; repeated entries count once. `block_table`: each sequence block is held by exactly one storage block, and sequence blocks b and 31 - b are held by the same ctx index.
All inputs are finite; a program needn't handle non-finite values.
Results may differ from the reference program's by a relative error of at most 0.015.
Values may be sent and summed in bfloat16 or wider, within the bound.
No kernel may reach another device: no remote copies, remote signals or barrier semaphores. Data moves between devices by JAX's collectives and lax.ppermute only.
A program may use at most 64 MiB of HBM per device.

```python
import jax
import jax.numpy as jnp
from jax import lax

QUERY_HEADS = 64
KEY_VALUE_HEADS = 8
HEAD_SIZE = 128
BLK = 128
KMAX = 10
BLK_DEV = 2
SEQUENCE_BLOCKS = 32
EPISODE_TOKENS = 4096
N_CTX = 16


def draw_query_rows(key, part):
    row_count = SEQUENCE_BLOCKS * BLK
    complete_shape = (row_count, KEY_VALUE_HEADS, QUERY_HEADS // KEY_VALUE_HEADS, HEAD_SIZE)
    sampled_values = jnp.clip(jax.random.normal(jax.random.fold_in(key, 11), complete_shape, jnp.float32), -6.0, 6.0)
    return sampled_values.reshape(row_count, QUERY_HEADS * HEAD_SIZE).astype(jnp.bfloat16)


def draw_key_rows(key, part):
    row_count = SEQUENCE_BLOCKS * BLK
    complete_shape = (row_count, KEY_VALUE_HEADS, HEAD_SIZE)
    sampled_values = jnp.clip(jax.random.normal(jax.random.fold_in(key, 13), complete_shape, jnp.float32), -4.0, 4.0)
    return sampled_values.reshape(row_count, KEY_VALUE_HEADS * HEAD_SIZE).astype(jnp.bfloat16)


def draw_block_table(key, part):
    order = jax.random.permutation(jax.random.fold_in(key, 17), SEQUENCE_BLOCKS // 2).astype(jnp.int32)
    lower = order.reshape(N_CTX, BLK_DEV // 2)
    upper = SEQUENCE_BLOCKS - 1 - lower
    return jnp.concatenate([lower, upper], axis=1).astype(jnp.int32)


def draw_pattern(key, part):
    block_ids = jnp.arange(SEQUENCE_BLOCKS, dtype=jnp.int32)
    fixed_part = jnp.stack([block_ids, jnp.maximum(block_ids - 1, 0), jnp.zeros_like(block_ids)], axis=1)
    random_part = jax.random.randint(jax.random.fold_in(key, 19), (SEQUENCE_BLOCKS, KMAX - 3), 0, (block_ids + 1)[:, None], dtype=jnp.int32)
    return jnp.concatenate([fixed_part, random_part], axis=1).astype(jnp.int32)


def level_of(stream_key, shape, split, least, largest):
    loudness, own = 1.0, jax.random.fold_in(stream_key, 6)
    for dim, shards_of in split:
        draws = jnp.exp(jax.random.uniform(jax.random.fold_in(own, dim), (shards_of,), jnp.float32, least / len(split), largest / len(split)))
        loudness = loudness * jnp.repeat(draws, shape[dim] // shards_of).reshape([-1 if axis == dim else 1 for axis in range(len(shape))])
    return loudness


def scatter_about(rng, extent, deviation, most, pieces=(), kind=jnp.bfloat16):
    values = deviation * jax.random.normal(rng, extent, jnp.float32)
    if pieces:
        values = values * level_of(rng, extent, pieces, -0.22, 0.18)
    return jnp.clip(values, -most, most).astype(kind)


def setup_inputs(seed: int = 0, part: int = 0) -> dict:
    seeds = jax.random.split(jax.random.key(seed), 7)
    part_splits = jax.random.split(jax.random.fold_in(seeds[6], part), 7)
    return {
        "query_rows": draw_query_rows(jax.random.fold_in(jax.random.fold_in(seeds[6], part), 71), part),
        "key_rows": draw_key_rows(jax.random.fold_in(jax.random.fold_in(seeds[6], part), 71), part),
        "stored_value_rows": scatter_about(part_splits[2], (EPISODE_TOKENS, KEY_VALUE_HEADS * HEAD_SIZE), 1.0, 6.0, ((0, 16), (1, 8))),
        "out_grad": scatter_about(part_splits[3], (EPISODE_TOKENS, QUERY_HEADS * HEAD_SIZE), 1.0, 6.0, ((0, 16), (1, 8))),
        "block_table": draw_block_table(jax.random.fold_in(jax.random.fold_in(seeds[6], part), 71), part),
        "pattern": draw_pattern(jax.random.fold_in(jax.random.fold_in(seeds[6], part), 71), part),
    }


def slot_layout(block_table, pattern, held_seq):
    blocks = pattern.shape[0]
    slots = pattern.shape[1]
    block_ids = jnp.arange(blocks, dtype=jnp.int32)
    store_seq = block_table.reshape(-1)
    inverse = jnp.sum(jnp.where(store_seq[:, None] == block_ids[None, :], block_ids[:, None], 0), axis=0).astype(jnp.int32)
    onehot = (held_seq[:, None] == block_ids[None, :]).astype(jnp.int32)
    held_pattern = jnp.sum(onehot[:, :, None] * pattern[None, :, :], axis=1).astype(jnp.int32)
    key_store = jnp.sum(jnp.where(held_pattern[:, :, None] == block_ids[None, None, :], inverse[None, None, :], 0), axis=2).astype(jnp.int32)
    same = held_pattern[:, :, None] == held_pattern[:, None, :]
    slot_ids = jnp.arange(slots, dtype=jnp.int32)
    before = slot_ids[None, :] < slot_ids[:, None]
    live_slot = jnp.logical_not(jnp.any(same & before[None], axis=2))
    inner = jnp.arange(BLK, dtype=jnp.int32)
    query_pos = held_seq[:, None] * BLK + inner[None, :]
    key_pos = held_pattern[:, :, None] * BLK + inner[None, None, :]
    allowed = live_slot[:, None, :, None] & (key_pos[:, None, :, :] <= query_pos[:, :, None, None])
    return key_store, allowed


def attend_tiles(query_held, grad_held, key_tiles, value_tiles, allowed):
    scaling = HEAD_SIZE ** -0.5
    query_wide = query_held.astype(jnp.float32)
    grad_wide = grad_held.astype(jnp.float32)
    key_wide = key_tiles.astype(jnp.float32)
    value_wide = value_tiles.astype(jnp.float32)
    scores = jnp.einsum('biagd,bjkad->bagijk', query_wide, key_wide) * scaling
    scores = jnp.where(allowed[:, None, None], scores, -jnp.inf)
    row_max = jnp.max(scores, axis=(4, 5), keepdims=True)
    row_sum = jnp.sum(jnp.exp(scores - row_max), axis=(4, 5), keepdims=True)
    log_total = row_max + jnp.log(row_sum)
    prob_full = jnp.exp(scores - log_total)
    prob_low = prob_full.astype(jnp.bfloat16)
    attended_wide = jnp.einsum('bagijk,bjkad->biagd', prob_low.astype(jnp.float32), value_wide)
    attended = attended_wide.astype(jnp.bfloat16)
    row_dot = jnp.sum(grad_wide * attended_wide, axis=-1)
    row_dot = jnp.transpose(row_dot, (0, 2, 3, 1))[..., None, None]
    grad_prob = jnp.einsum('biagd,bjkad->bagijk', grad_wide, value_wide)
    grad_score = (prob_full * (grad_prob - row_dot) * scaling).astype(jnp.bfloat16)
    query_grad = jnp.einsum('bagijk,bjkad->biagd', grad_score.astype(jnp.float32), key_wide).astype(jnp.bfloat16)
    key_grads = jnp.einsum('bagijk,biagd->bjkad', grad_score.astype(jnp.float32), query_wide)
    value_grads = jnp.einsum('bagijk,biagd->bjkad', prob_low.astype(jnp.float32), grad_wide)
    return attended, query_grad, key_grads, value_grads


def reference(query_rows, key_rows, stored_value_rows, out_grad, block_table, pattern):
    blocks = pattern.shape[0]
    row_count = query_rows.shape[0]
    per_dev = block_table.shape[1]
    kv_heads = key_rows.shape[1] // HEAD_SIZE
    groups = query_rows.shape[1] // key_rows.shape[1]
    key_blocks = key_rows.reshape(blocks, BLK, kv_heads, HEAD_SIZE)
    value_blocks = stored_value_rows.reshape(blocks, BLK, kv_heads, HEAD_SIZE)

    def one_device(running, device):
        key_sums, value_sums = running
        held_seq = block_table[device]
        key_store, allowed = slot_layout(block_table, pattern, held_seq)
        first_row = (device * per_dev * BLK).astype(jnp.int32)
        query_held = lax.dynamic_slice_in_dim(query_rows, first_row, per_dev * BLK, 0).reshape(per_dev, BLK, kv_heads, groups, HEAD_SIZE)
        grad_held = lax.dynamic_slice_in_dim(out_grad, first_row, per_dev * BLK, 0).reshape(per_dev, BLK, kv_heads, groups, HEAD_SIZE)
        key_tiles = key_blocks[key_store]
        value_tiles = value_blocks[key_store]
        attended, query_grad, key_grads, value_grads = attend_tiles(query_held, grad_held, key_tiles, value_tiles, allowed)
        flat_slots = key_store.reshape(-1)
        key_partial = jnp.zeros((blocks, BLK, kv_heads, HEAD_SIZE), jnp.float32).at[flat_slots].add(key_grads.reshape(-1, BLK, kv_heads, HEAD_SIZE))
        value_partial = jnp.zeros((blocks, BLK, kv_heads, HEAD_SIZE), jnp.float32).at[flat_slots].add(value_grads.reshape(-1, BLK, kv_heads, HEAD_SIZE))
        key_low = lax.optimization_barrier(key_partial.astype(jnp.bfloat16))
        value_low = lax.optimization_barrier(value_partial.astype(jnp.bfloat16))
        key_sums = key_sums + key_low.astype(jnp.float32)
        value_sums = value_sums + value_low.astype(jnp.float32)
        return (key_sums, value_sums), (attended, query_grad)

    start = (jnp.zeros((blocks, BLK, kv_heads, HEAD_SIZE), jnp.float32), jnp.zeros((blocks, BLK, kv_heads, HEAD_SIZE), jnp.float32))
    (key_sums, value_sums), (attended, query_grad) = lax.scan(one_device, start, jnp.arange(N_CTX, dtype=jnp.int32))
    attended = attended.reshape(row_count, -1)
    query_grad = query_grad.reshape(row_count, -1)
    key_grad = key_sums.reshape(row_count, -1).astype(jnp.bfloat16)
    value_grad = value_sums.reshape(row_count, -1).astype(jnp.bfloat16)
    return (attended, query_grad, key_grad, value_grad)
```

```python
import math

import jax
import jax.numpy as jnp
from jax import lax
from jax.experimental import pallas as pl
from jax.experimental.pallas import tpu as pltpu
from jax.sharding import Mesh, PartitionSpec as P

D = 128
BLK = 128
NX, NY, NC = 4, 2, 2
NEG = -1e30
SWAP = [(0, 1), (1, 0)]


def slot_tables(block_table, pattern, held_seq, my_y, my_core):
    blocks = pattern.shape[0]
    slots = pattern.shape[1]
    block_ids = jnp.arange(blocks, dtype=jnp.int32)
    store_seq = block_table.reshape(-1)
    inverse = jnp.sum(
        jnp.where(store_seq[:, None] == block_ids[None, :], block_ids[:, None], 0), axis=0
    )
    onehot = (held_seq[:, None] == block_ids[None, :]).astype(jnp.int32)
    held_pattern = jnp.sum(onehot[:, :, None] * pattern[None, :, :], axis=1)
    store = jnp.sum(
        jnp.where(held_pattern[:, :, None] == block_ids[None, None, :], inverse[None, None, :], 0),
        axis=2,
    )
    same = held_pattern[:, :, None] == held_pattern[:, None, :]
    slot_ids = jnp.arange(slots, dtype=jnp.int32)
    before = slot_ids[None, :] < slot_ids[:, None]
    live = jnp.logical_not(jnp.any(same & before[None], axis=2)).astype(jnp.int32)
    diag = (held_pattern == held_seq[:, None]).astype(jnp.int32)
    sub = store % 2
    dev = store // 2
    core = dev % 2
    yh = (dev // 2) % 2
    xi = dev // 4
    half = jnp.bitwise_xor(core, my_core)
    row = xi * 1024 + jnp.bitwise_xor(yh, my_y) * 512 + sub * BLK
    kind = live * (1 + diag)
    return jnp.concatenate([half.reshape(-1), row.reshape(-1), kind.reshape(-1)]).astype(jnp.int32)


def attend_kernel(
    tab, q_ref, g_ref, kva_ref, kvb_ref,
    att_ref, qg_ref, pa_ref, pb_ref,
    kg, vg, bias, p_sc, ds_sc, qs, gs, acc_a, acc_b,
):
    nslot = kg.shape[0] // BLK
    heads = q_ref.shape[1] // D
    scale = D ** -0.5
    c2 = scale * math.log2(math.e)
    per = q_ref.shape[0] // BLK
    ns = per * nslot
    acc_a[...] = jnp.zeros_like(acc_a)
    acc_b[...] = jnp.zeros_like(acc_b)

    def one_block(b, _):
        r0 = pl.multiple_of(b * BLK, BLK)
        for j in range(nslot):
            t = b * nslot + j
            half = tab[t]
            row = pl.multiple_of(tab[ns + t], BLK)
            kind = tab[2 * ns + t]
            dst = pl.ds(j * BLK, BLK)

            @pl.when(half == 0)
            def _():
                kg[dst, :] = kva_ref[pl.ds(row, BLK), :]
                vg[dst, :] = kva_ref[pl.ds(row + 256, BLK), :]

            @pl.when(half == 1)
            def _():
                kg[dst, :] = kvb_ref[pl.ds(row, BLK), :]
                vg[dst, :] = kvb_ref[pl.ds(row + 256, BLK), :]

            ri = lax.broadcasted_iota(jnp.int32, (BLK, BLK), 0)
            ci = lax.broadcasted_iota(jnp.int32, (BLK, BLK), 1)
            ok = jnp.logical_or(ci <= ri, kind != 2)
            ok = jnp.logical_and(ok, kind > 0)
            bias[:, j * BLK:(j + 1) * BLK] = jnp.where(ok, 0.0, NEG)

        def one_head(h, _):
            h0 = pl.multiple_of(h * D, D)
            q = q_ref[pl.ds(r0, BLK), pl.ds(h0, D)]
            g = g_ref[pl.ds(r0, BLK), pl.ds(h0, D)]
            qs[pl.ds(h0, BLK), :] = q
            gs[pl.ds(h0, BLK), :] = g
            k = kg[...]
            v = vg[...]
            nt = (((1,), (1,)), ((), ()))
            s = lax.dot_general(q, k, nt, preferred_element_type=jnp.float32)
            s = s * c2 + bias[...]
            m = jnp.max(s, axis=1, keepdims=True)
            e = jnp.exp2(s - m)
            inv = 1.0 / jnp.sum(e, axis=1, keepdims=True)
            prob = e * inv
            low = prob.astype(jnp.bfloat16)
            p_sc[pl.ds(h0, BLK), :] = low
            wide = jnp.dot(low, v, preferred_element_type=jnp.float32)
            att_ref[pl.ds(r0, BLK), pl.ds(h0, D)] = wide.astype(jnp.bfloat16)
            rd = jnp.sum(g.astype(jnp.float32) * wide, axis=1, keepdims=True)
            gp = lax.dot_general(g, v, nt, preferred_element_type=jnp.float32)
            ds = (prob * ((gp - rd) * scale)).astype(jnp.bfloat16)
            ds_sc[pl.ds(h0, BLK), :] = ds
            qg = jnp.dot(ds, k, preferred_element_type=jnp.float32)
            qg_ref[pl.ds(r0, BLK), pl.ds(h0, D)] = qg.astype(jnp.bfloat16)
            return 0

        lax.fori_loop(0, heads, one_head, 0)
        tn = (((0,), (0,)), ((), ()))
        for j0 in range(0, nslot, 2):
            w = pl.ds(j0 * BLK, 2 * BLK)
            dk = lax.dot_general(ds_sc[:, w], qs[...], tn, preferred_element_type=jnp.float32)
            dv = lax.dot_general(p_sc[:, w], gs[...], tn, preferred_element_type=jnp.float32)
            for i in range(2):
                t = b * nslot + j0 + i
                half = tab[t]
                row = pl.multiple_of(tab[ns + t], BLK)
                rows_k = pl.ds(row, BLK)
                rows_v = pl.ds(row + 256, BLK)
                dk_i = dk[i * BLK:(i + 1) * BLK]
                dv_i = dv[i * BLK:(i + 1) * BLK]

                @pl.when(half == 0)
                def _():
                    acc_a[rows_k, :] += dk_i
                    acc_a[rows_v, :] += dv_i

                @pl.when(half == 1)
                def _():
                    acc_b[rows_k, :] += dk_i
                    acc_b[rows_v, :] += dv_i
        return 0

    lax.fori_loop(0, per, one_block, 0)
    pa_ref[...] = acc_a[...].astype(jnp.bfloat16)
    pb_ref[...] = acc_b[...].astype(jnp.bfloat16)


def attend(tab, q, g, kva, kvb, nslot):
    rows, cols = q.shape
    heads = cols // D
    half_rows = kva.shape[0]
    bf = jnp.bfloat16
    vm = pl.BlockSpec(memory_space=pltpu.VMEM)
    return pl.pallas_call(
        attend_kernel,
        out_shape=(
            jax.ShapeDtypeStruct((rows, cols), bf),
            jax.ShapeDtypeStruct((rows, cols), bf),
            jax.ShapeDtypeStruct((half_rows, D), bf),
            jax.ShapeDtypeStruct((half_rows, D), bf),
        ),
        in_specs=[pl.BlockSpec(memory_space=pltpu.SMEM), vm, vm, vm, vm],
        out_specs=(vm, vm, vm, vm),
        scratch_shapes=[
            pltpu.VMEM((nslot * BLK, D), bf),
            pltpu.VMEM((nslot * BLK, D), bf),
            pltpu.VMEM((BLK, nslot * BLK), jnp.float32),
            pltpu.VMEM((heads * BLK, nslot * BLK), bf),
            pltpu.VMEM((heads * BLK, nslot * BLK), bf),
            pltpu.VMEM((heads * BLK, D), bf),
            pltpu.VMEM((heads * BLK, D), bf),
            pltpu.VMEM((half_rows, D), jnp.float32),
            pltpu.VMEM((half_rows, D), jnp.float32),
        ],
        compiler_params=pltpu.CompilerParams(vmem_limit_bytes=48 << 20),
        name="attend",
    )(tab, q, g, kva, kvb)


def per_device(query_rows, key_rows, value_rows, out_grad, block_table, pattern):
    my_x = lax.axis_index("x")
    my_y = lax.axis_index("yh")
    my_core = lax.axis_index("core")
    ctx = my_x * (NY * NC) + my_y * NC + my_core
    held_seq = lax.dynamic_index_in_dim(block_table, ctx, 0, keepdims=False)
    f32 = jnp.float32
    bf = jnp.bfloat16
    own = jnp.concatenate([key_rows, value_rows], axis=0)
    peer = lax.ppermute(own, "yh", SWAP)
    pair = jnp.concatenate([own, peer], axis=0)
    n = pair.shape[0]
    kva = lax.all_to_all(
        jnp.broadcast_to(pair[None], (NX, n, D)), "x", 0, 0, tiled=True
    ).reshape(NX * n, D)
    kvb = lax.ppermute(kva, "core", SWAP)
    tab = slot_tables(block_table, pattern, held_seq, my_y, my_core)
    attended, query_grad, part_a, part_b = attend(
        tab, query_rows, out_grad, kva, kvb, pattern.shape[1]
    )
    other = lax.ppermute(part_b, "core", SWAP)
    both = (part_a.astype(f32) + other.astype(f32)).astype(bf).reshape(NX, n, D)
    from_x = lax.all_to_all(both, "x", 0, 0, tiled=True)
    over_x = jnp.sum(from_x.astype(f32), axis=0)
    from_y = lax.ppermute(over_x[n // 2:].astype(bf), "yh", SWAP)
    total = (over_x[: n // 2] + from_y.astype(f32)).astype(bf)
    return attended, query_grad, total[: n // 4], total[n // 4:]


def solution(mesh):
    dp, head = mesh.shape["dp"], mesh.shape["head"]
    fine = Mesh(mesh.devices.reshape(dp, head, NX, NY, NC), ("dp", "head", "x", "yh", "core"))
    rows = P(("dp", "x", "yh", "core"), "head")
    return jax.shard_map(
        per_device,
        mesh=fine,
        in_specs=(rows, rows, rows, rows, P("dp", None), P("dp", None)),
        out_specs=(rows, rows, rows, rows),
        check_vma=False,
    )
```

```python
import math

import jax
import jax.numpy as jnp
from jax import lax
from jax.experimental import pallas as pl
from jax.experimental.pallas import tpu as pltpu
from jax.sharding import Mesh, PartitionSpec as P

D = 128
BLK = 128
NX, NY, NC = 4, 2, 2
NEG = -1e30
RC = 16
VMEM_PARTS = 28
VMEM_ROWS = 16
SWAP = [(0, 1), (1, 0)]


def slot_tables(block_table, pattern, held_seq, my_y, my_core):
    blocks = pattern.shape[0]
    slots = pattern.shape[1]
    block_ids = jnp.arange(blocks, dtype=jnp.int32)
    store_seq = block_table.reshape(-1)
    inverse = jnp.sum(
        jnp.where(store_seq[:, None] == block_ids[None, :], block_ids[:, None], 0), axis=0
    )
    onehot = (held_seq[:, None] == block_ids[None, :]).astype(jnp.int32)
    held_pattern = jnp.sum(onehot[:, :, None] * pattern[None, :, :], axis=1)
    store = jnp.sum(
        jnp.where(held_pattern[:, :, None] == block_ids[None, None, :], inverse[None, None, :], 0),
        axis=2,
    )
    same = held_pattern[:, :, None] == held_pattern[:, None, :]
    slot_ids = jnp.arange(slots, dtype=jnp.int32)
    before = slot_ids[None, :] < slot_ids[:, None]
    live = jnp.logical_not(jnp.any(same & before[None], axis=2)).astype(jnp.int32)
    diag = (held_pattern == held_seq[:, None]).astype(jnp.int32)
    sub = store % 2
    dev = store // 2
    core = dev % 2
    yh = (dev // 2) % 2
    xi = dev // 4
    half = jnp.bitwise_xor(core, my_core)
    row = xi * 1024 + yh * 512 + sub * BLK
    part_row = xi * 1024 + jnp.bitwise_xor(yh, my_y) * 512 + sub * BLK
    kind = live * (1 + diag)
    tables = [half, row, kind, part_row]
    return jnp.concatenate([t.reshape(-1) for t in tables]).astype(jnp.int32)


def load_keys(b, nslot, ns, tab, kva_ref, kvb_ref, kg, vg):
    for j in range(nslot):
        t = b * nslot + j
        half = tab[t]
        row = pl.multiple_of(tab[ns + t], BLK)
        dst = pl.ds(j * BLK, BLK)

        @pl.when(half == 0)
        def _():
            kg[dst, :] = kva_ref[pl.ds(row, BLK), :]
            vg[dst, :] = kva_ref[pl.ds(row + 256, BLK), :]

        @pl.when(half == 1)
        def _():
            kg[dst, :] = kvb_ref[pl.ds(row, BLK), :]
            vg[dst, :] = kvb_ref[pl.ds(row + 256, BLK), :]


def part_kernel(
    tab, q_ref, g_ref, kva_ref, kvb_ref, pa_ref, pb_ref, p_ref, ds_ref,
    kg, vg, bias, qs, gs, s_sc, gp_sc, p_sc, ds_sc, acc_a, acc_b,
):
    nslot = kg.shape[0] // BLK
    per = q_ref.shape[0] // BLK
    ns = per * nslot
    heads = q_ref.shape[1] // D
    stacked = heads * BLK
    scale = D ** -0.5
    c2 = scale * math.log2(math.e)
    nt = (((1,), (1,)), ((), ()))
    tn = (((0,), (0,)), ((), ()))
    acc_a[...] = jnp.zeros_like(acc_a)
    acc_b[...] = jnp.zeros_like(acc_b)

    def one_block(b, _):
        r0 = pl.multiple_of(b * BLK, BLK)
        s0 = pl.multiple_of(b * stacked, stacked)
        load_keys(b, nslot, ns, tab, kva_ref, kvb_ref, kg, vg)
        for j in range(nslot):
            kind = tab[2 * ns + b * nslot + j]
            ri = lax.broadcasted_iota(jnp.int32, (BLK, BLK), 0)
            ci = lax.broadcasted_iota(jnp.int32, (BLK, BLK), 1)
            ok = jnp.logical_or(ci <= ri, kind != 2)
            ok = jnp.logical_and(ok, kind > 0)
            bias[:, j * BLK:(j + 1) * BLK] = jnp.where(ok, 0.0, NEG)
        for h in range(heads):
            qs[h * BLK:(h + 1) * BLK, :] = q_ref[pl.ds(r0, BLK), h * D:(h + 1) * D]
            gs[h * BLK:(h + 1) * BLK, :] = g_ref[pl.ds(r0, BLK), h * D:(h + 1) * D]
        s_sc[...] = lax.dot_general(qs[...], kg[...], nt, preferred_element_type=jnp.float32)
        gp_sc[...] = lax.dot_general(gs[...], vg[...], nt, preferred_element_type=jnp.float32)
        for r in range(0, stacked, RC):
            rr = slice(r, r + RC)
            out = pl.ds(s0 + r, RC)
            s = s_sc[rr, :] * c2 + bias[r % BLK:r % BLK + RC, :]
            m = jnp.max(s, axis=1, keepdims=True)
            e = jnp.exp2(s - m)
            prob = e * (1.0 / jnp.sum(e, axis=1, keepdims=True))
            p_sc[rr, :] = prob.astype(jnp.bfloat16)
            gp = gp_sc[rr, :]
            rd = jnp.sum(prob * gp, axis=1, keepdims=True)
            ds_sc[rr, :] = (prob * (gp - rd)).astype(jnp.bfloat16)
        mine = pl.ds(s0, stacked)
        p_ref[mine, :] = p_sc[...]
        ds_ref[mine, :] = ds_sc[...]
        dk_all = lax.dot_general(ds_sc[...], qs[...], tn, preferred_element_type=jnp.float32) * scale
        dv_all = lax.dot_general(p_sc[...], gs[...], tn, preferred_element_type=jnp.float32)
        for j in range(nslot):
            t = b * nslot + j
            half = tab[t]
            row = pl.multiple_of(tab[3 * ns + t], BLK)
            rows_k = pl.ds(row, BLK)
            rows_v = pl.ds(row + 256, BLK)
            dk_j = dk_all[j * BLK:(j + 1) * BLK]
            dv_j = dv_all[j * BLK:(j + 1) * BLK]

            @pl.when(half == 0)
            def _():
                acc_a[rows_k, :] += dk_j
                acc_a[rows_v, :] += dv_j

            @pl.when(half == 1)
            def _():
                acc_b[rows_k, :] += dk_j
                acc_b[rows_v, :] += dv_j
        return 0

    lax.fori_loop(0, per, one_block, 0)
    pa_ref[...] = acc_a[...].astype(jnp.bfloat16)
    pb_ref[...] = acc_b[...].astype(jnp.bfloat16)


def row_kernel(tab, p_ref, ds_ref, kva_ref, kvb_ref, att_ref, qg_ref, kg, vg):
    nslot = kg.shape[0] // BLK
    per = att_ref.shape[0] // BLK
    heads = att_ref.shape[1] // D
    stacked = heads * BLK
    scale = D ** -0.5

    def one_block(b, _):
        load_keys(b, nslot, per * nslot, tab, kva_ref, kvb_ref, kg, vg)
        r0 = pl.multiple_of(b * BLK, BLK)
        mine = pl.ds(pl.multiple_of(b * stacked, stacked), stacked)
        wide = jnp.dot(p_ref[mine, :], vg[...], preferred_element_type=jnp.float32)
        qg = jnp.dot(ds_ref[mine, :], kg[...], preferred_element_type=jnp.float32) * scale
        for h in range(heads):
            cols = slice(h * D, (h + 1) * D)
            hr = slice(h * BLK, (h + 1) * BLK)
            att_ref[pl.ds(r0, BLK), cols] = wide[hr].astype(jnp.bfloat16)
            qg_ref[pl.ds(r0, BLK), cols] = qg[hr].astype(jnp.bfloat16)
        return 0

    lax.fori_loop(0, per, one_block, 0)


VM = pl.BlockSpec(memory_space=pltpu.VMEM)
SM = pl.BlockSpec(memory_space=pltpu.SMEM)


def parts(tab, q, g, kva, kvb, nslot):
    per = q.shape[0] // BLK
    stacked = q.shape[1] // D * BLK
    bf, f32 = jnp.bfloat16, jnp.float32
    keys = nslot * BLK
    shapes = (kva.shape, kvb.shape, (per * stacked, keys), (per * stacked, keys))
    work = per * stacked * keys
    return pl.pallas_call(
        part_kernel,
        out_shape=tuple(jax.ShapeDtypeStruct(s, bf) for s in shapes),
        in_specs=[SM, VM, VM, VM, VM],
        out_specs=(VM, VM, VM, VM),
        scratch_shapes=[
            pltpu.VMEM((keys, D), bf),
            pltpu.VMEM((keys, D), bf),
            pltpu.VMEM((BLK, keys), f32),
            pltpu.VMEM((stacked, D), bf),
            pltpu.VMEM((stacked, D), bf),
            pltpu.VMEM((stacked, keys), f32),
            pltpu.VMEM((stacked, keys), f32),
            pltpu.VMEM((stacked, keys), bf),
            pltpu.VMEM((stacked, keys), bf),
            pltpu.VMEM(kva.shape, f32),
            pltpu.VMEM(kvb.shape, f32),
        ],
        compiler_params=pltpu.CompilerParams(vmem_limit_bytes=VMEM_PARTS << 20),
        cost_estimate=pl.CostEstimate(
            flops=8 * D * work, transcendentals=work, bytes_accessed=6 << 20
        ),
        name="parts",
    )(tab, q, g, kva, kvb)


def rows(tab, p, ds, kva, kvb, shape, nslot):
    bf = jnp.bfloat16
    keys = nslot * BLK
    return pl.pallas_call(
        row_kernel,
        out_shape=tuple(jax.ShapeDtypeStruct(shape, bf) for _ in range(2)),
        in_specs=[SM, VM, VM, VM, VM],
        out_specs=(VM, VM),
        scratch_shapes=[pltpu.VMEM((keys, D), bf), pltpu.VMEM((keys, D), bf)],
        compiler_params=pltpu.CompilerParams(vmem_limit_bytes=VMEM_ROWS << 20),
        cost_estimate=pl.CostEstimate(
            flops=4 * D * p.shape[0] * keys, transcendentals=0, bytes_accessed=6 << 20
        ),
        name="rows",
    )(tab, p, ds, kva, kvb)


def per_device(query_rows, key_rows, value_rows, out_grad, block_table, pattern):
    my_x = lax.axis_index("x")
    my_y = lax.axis_index("yh")
    my_core = lax.axis_index("core")
    ctx = my_x * (NY * NC) + my_y * NC + my_core
    held_seq = lax.dynamic_index_in_dim(block_table, ctx, 0, keepdims=False)
    f32 = jnp.float32
    bf = jnp.bfloat16
    own = jnp.concatenate([key_rows, value_rows], axis=0)
    pair = lax.all_gather(own, "yh", axis=0, tiled=True)
    n = pair.shape[0]
    kva = lax.all_to_all(
        jnp.broadcast_to(pair[None], (NX, n, D)), "x", 0, 0, tiled=True
    ).reshape(NX * n, D)
    kvb = lax.ppermute(kva, "core", SWAP)
    tab = slot_tables(block_table, pattern, held_seq, my_y, my_core)
    nslot = pattern.shape[1]
    part_a, part_b, prob, grad_score = parts(tab, query_rows, out_grad, kva, kvb, nslot)
    other = lax.ppermute(part_b, "core", SWAP)
    both = (part_a.astype(f32) + other.astype(f32)).astype(bf).reshape(NX, n, D)
    both, prob, grad_score = lax.optimization_barrier((both, prob, grad_score))
    attended, query_grad = rows(tab, prob, grad_score, kva, kvb, query_rows.shape, nslot)
    from_x = lax.all_to_all(both, "x", 0, 0, tiled=True)
    over_x = jnp.sum(from_x.astype(f32), axis=0)
    from_y = lax.ppermute(over_x[n // 2:].astype(bf), "yh", SWAP)
    total = (over_x[: n // 2] + from_y.astype(f32)).astype(bf)
    return attended, query_grad, total[: n // 4], total[n // 4:]


def solution(mesh):
    dp, head = mesh.shape["dp"], mesh.shape["head"]
    fine = Mesh(mesh.devices.reshape(dp, head, NX, NY, NC), ("dp", "head", "x", "yh", "core"))
    spec = P(("dp", "x", "yh", "core"), "head")
    return jax.shard_map(
        per_device,
        mesh=fine,
        in_specs=(spec, spec, spec, spec, P("dp", None), P("dp", None)),
        out_specs=(spec, spec, spec, spec),
        check_vma=False,
    )
```

```python
import math

import jax
import jax.numpy as jnp
from jax import lax
from jax.experimental import pallas as pl
from jax.experimental.pallas import tpu as pltpu
from jax.sharding import Mesh, PartitionSpec as P

D = 128
BLK = 128
NX, NY, NC = 4, 2, 2
NEG = -1e30
RC = 16
VMEM_PARTS = 28
VMEM_ROWS = 16
SWAP = [(0, 1), (1, 0)]


def fill_tables(place, bt, pat, inv, tab):
    per, devs = bt.shape
    nslot = pat.shape[0]
    ns = per * nslot
    ctx, my_y, my_core = (place[i] for i in range(3))
    for dev in range(devs):
        for sub in range(per):
            inv[bt[sub, dev]] = dev * per + sub
    for b in range(per):
        seq = bt[b, ctx]
        keys = [pat[j, seq] for j in range(nslot)]
        for j in range(nslot):
            dead = jnp.int32(0)
            for i in range(j):
                dead = dead | (keys[i] == keys[j]).astype(jnp.int32)
            store = inv[keys[j]]
            sub = store & 1
            core = (store >> 1) & 1
            yh = (store >> 2) & 1
            xi = store >> 3
            away = yh ^ my_y
            t = b * nslot + j
            tab[t] = core ^ my_core
            tab[ns + t] = xi * 1024 + yh * 512 + sub * BLK
            tab[2 * ns + t] = (1 - dead) * (1 + (keys[j] == seq).astype(jnp.int32))
            tab[3 * ns + t] = xi * 1024 + away * 512 + sub * BLK


def load_keys(b, nslot, ns, tab, kva_ref, kvb_ref, kg, vg):
    for j in range(nslot):
        t = b * nslot + j
        half = tab[t]
        row = pl.multiple_of(tab[ns + t], BLK)
        dst = pl.ds(j * BLK, BLK)

        @pl.when(half == 0)
        def _():
            kg[dst, :] = kva_ref[pl.ds(row, BLK), :]
            vg[dst, :] = kva_ref[pl.ds(row + 256, BLK), :]

        @pl.when(half == 1)
        def _():
            kg[dst, :] = kvb_ref[pl.ds(row, BLK), :]
            vg[dst, :] = kvb_ref[pl.ds(row + 256, BLK), :]


def part_kernel(
    place, bt, pat, q_ref, g_ref, kva_ref, kvb_ref, pa_ref, pb_ref, p_ref, ds_ref,
    kg, vg, bias, qs, gs, s_sc, gp_sc, p_sc, ds_sc, acc_a, acc_b, inv, tab,
):
    nslot = kg.shape[0] // BLK
    per = q_ref.shape[0] // BLK
    ns = per * nslot
    heads = q_ref.shape[1] // D
    stacked = heads * BLK
    scale = D ** -0.5
    c2 = scale * math.log2(math.e)
    nt = (((1,), (1,)), ((), ()))
    tn = (((0,), (0,)), ((), ()))
    fill_tables(place, bt, pat, inv, tab)
    acc_a[...] = jnp.zeros_like(acc_a)
    acc_b[...] = jnp.zeros_like(acc_b)

    def one_block(b, _):
        r0 = pl.multiple_of(b * BLK, BLK)
        s0 = pl.multiple_of(b * stacked, stacked)
        load_keys(b, nslot, ns, tab, kva_ref, kvb_ref, kg, vg)
        for j in range(nslot):
            kind = tab[2 * ns + b * nslot + j]
            ri = lax.broadcasted_iota(jnp.int32, (BLK, BLK), 0)
            ci = lax.broadcasted_iota(jnp.int32, (BLK, BLK), 1)
            ok = jnp.logical_or(ci <= ri, kind != 2)
            ok = jnp.logical_and(ok, kind > 0)
            bias[:, j * BLK:(j + 1) * BLK] = jnp.where(ok, 0.0, NEG)
        for h in range(heads):
            qs[h * BLK:(h + 1) * BLK, :] = q_ref[pl.ds(r0, BLK), h * D:(h + 1) * D]
            gs[h * BLK:(h + 1) * BLK, :] = g_ref[pl.ds(r0, BLK), h * D:(h + 1) * D]
        s_sc[...] = lax.dot_general(qs[...], kg[...], nt, preferred_element_type=jnp.float32)
        gp_sc[...] = lax.dot_general(gs[...], vg[...], nt, preferred_element_type=jnp.float32)
        for r in range(0, stacked, RC):
            rr = slice(r, r + RC)
            out = pl.ds(s0 + r, RC)
            s = s_sc[rr, :] * c2 + bias[r % BLK:r % BLK + RC, :]
            m = jnp.max(s, axis=1, keepdims=True)
            e = jnp.exp2(s - m)
            prob = e * (1.0 / jnp.sum(e, axis=1, keepdims=True))
            p_sc[rr, :] = prob.astype(jnp.bfloat16)
            gp = gp_sc[rr, :]
            rd = jnp.sum(prob * gp, axis=1, keepdims=True)
            ds_sc[rr, :] = (prob * (gp - rd)).astype(jnp.bfloat16)
        mine = pl.ds(s0, stacked)
        p_ref[mine, :] = p_sc[...]
        ds_ref[mine, :] = ds_sc[...]
        dk_all = lax.dot_general(ds_sc[...], qs[...], tn, preferred_element_type=jnp.float32) * scale
        dv_all = lax.dot_general(p_sc[...], gs[...], tn, preferred_element_type=jnp.float32)
        for j in range(nslot):
            t = b * nslot + j
            half = tab[t]
            row = pl.multiple_of(tab[3 * ns + t], BLK)
            rows_k = pl.ds(row, BLK)
            rows_v = pl.ds(row + 256, BLK)
            dk_j = dk_all[j * BLK:(j + 1) * BLK]
            dv_j = dv_all[j * BLK:(j + 1) * BLK]

            @pl.when(half == 0)
            def _():
                acc_a[rows_k, :] += dk_j
                acc_a[rows_v, :] += dv_j

            @pl.when(half == 1)
            def _():
                acc_b[rows_k, :] += dk_j
                acc_b[rows_v, :] += dv_j
        return 0

    lax.fori_loop(0, per, one_block, 0)
    pa_ref[...] = acc_a[...].astype(jnp.bfloat16)
    pb_ref[...] = acc_b[...].astype(jnp.bfloat16)


def row_kernel(place, bt, pat, p_ref, ds_ref, kva_ref, kvb_ref, att_ref, qg_ref, kg, vg, inv, tab):
    nslot = kg.shape[0] // BLK
    per = att_ref.shape[0] // BLK
    heads = att_ref.shape[1] // D
    stacked = heads * BLK
    scale = D ** -0.5

    fill_tables(place, bt, pat, inv, tab)

    def one_block(b, _):
        load_keys(b, nslot, per * nslot, tab, kva_ref, kvb_ref, kg, vg)
        r0 = pl.multiple_of(b * BLK, BLK)
        mine = pl.ds(pl.multiple_of(b * stacked, stacked), stacked)
        wide = jnp.dot(p_ref[mine, :], vg[...], preferred_element_type=jnp.float32)
        qg = jnp.dot(ds_ref[mine, :], kg[...], preferred_element_type=jnp.float32) * scale
        for h in range(heads):
            cols = slice(h * D, (h + 1) * D)
            hr = slice(h * BLK, (h + 1) * BLK)
            att_ref[pl.ds(r0, BLK), cols] = wide[hr].astype(jnp.bfloat16)
            qg_ref[pl.ds(r0, BLK), cols] = qg[hr].astype(jnp.bfloat16)
        return 0

    lax.fori_loop(0, per, one_block, 0)


VM = pl.BlockSpec(memory_space=pltpu.VMEM)
SM = pl.BlockSpec(memory_space=pltpu.SMEM)


def parts(place, bt, pat, q, g, kva, kvb):
    nslot = pat.shape[0]
    per = q.shape[0] // BLK
    stacked = q.shape[1] // D * BLK
    bf, f32 = jnp.bfloat16, jnp.float32
    keys = nslot * BLK
    shapes = (kva.shape, kvb.shape, (per * stacked, keys), (per * stacked, keys))
    work = per * stacked * keys
    return pl.pallas_call(
        part_kernel,
        out_shape=tuple(jax.ShapeDtypeStruct(s, bf) for s in shapes),
        in_specs=[SM] * 3 + [VM] * 4,
        out_specs=(VM, VM, VM, VM),
        scratch_shapes=[
            pltpu.VMEM((keys, D), bf),
            pltpu.VMEM((keys, D), bf),
            pltpu.VMEM((BLK, keys), f32),
            pltpu.VMEM((stacked, D), bf),
            pltpu.VMEM((stacked, D), bf),
            pltpu.VMEM((stacked, keys), f32),
            pltpu.VMEM((stacked, keys), f32),
            pltpu.VMEM((stacked, keys), bf),
            pltpu.VMEM((stacked, keys), bf),
            pltpu.VMEM(kva.shape, f32),
            pltpu.VMEM(kvb.shape, f32),
            pltpu.SMEM((bt.shape[0] * bt.shape[1],), jnp.int32),
            pltpu.SMEM((4 * per * nslot,), jnp.int32),
        ],
        compiler_params=pltpu.CompilerParams(vmem_limit_bytes=VMEM_PARTS << 20),
        cost_estimate=pl.CostEstimate(
            flops=8 * D * work, transcendentals=work, bytes_accessed=6 << 20
        ),
        name="parts",
    )(place, bt, pat, q, g, kva, kvb)


def rows(place, bt, pat, p, ds, kva, kvb, shape):
    nslot = pat.shape[0]
    bf = jnp.bfloat16
    keys = nslot * BLK
    return pl.pallas_call(
        row_kernel,
        out_shape=tuple(jax.ShapeDtypeStruct(shape, bf) for _ in range(2)),
        in_specs=[SM] * 3 + [VM] * 4,
        out_specs=(VM, VM),
        scratch_shapes=[
            pltpu.VMEM((keys, D), bf),
            pltpu.VMEM((keys, D), bf),
            pltpu.SMEM((bt.shape[0] * bt.shape[1],), jnp.int32),
            pltpu.SMEM((4 * bt.shape[0] * nslot,), jnp.int32),
        ],
        compiler_params=pltpu.CompilerParams(vmem_limit_bytes=VMEM_ROWS << 20),
        cost_estimate=pl.CostEstimate(
            flops=4 * D * p.shape[0] * keys, transcendentals=0, bytes_accessed=6 << 20
        ),
        name="rows",
    )(place, bt, pat, p, ds, kva, kvb)


def per_device(query_rows, key_rows, value_rows, out_grad, block_table, pattern):
    my_x = lax.axis_index("x")
    my_y = lax.axis_index("yh")
    my_core = lax.axis_index("core")
    ctx = my_x * (NY * NC) + my_y * NC + my_core
    f32 = jnp.float32
    bf = jnp.bfloat16
    own = jnp.concatenate([key_rows, value_rows], axis=0)
    pair = lax.all_gather(own, "yh", axis=0, tiled=True)
    n = pair.shape[0]
    kva = lax.all_to_all(
        jnp.broadcast_to(pair[None], (NX, n, D)), "x", 0, 0, tiled=True
    ).reshape(NX * n, D)
    kvb = lax.ppermute(kva, "core", SWAP)
    place = jnp.stack([ctx, my_y, my_core]).astype(jnp.int32)
    bt, pat = block_table.T, pattern.T
    part_a, part_b, prob, grad_score = parts(place, bt, pat, query_rows, out_grad, kva, kvb)
    other = lax.ppermute(part_b, "core", SWAP)
    both = (part_a.astype(f32) + other.astype(f32)).astype(bf).reshape(NX, n, D)
    both, prob, grad_score = lax.optimization_barrier((both, prob, grad_score))
    attended, query_grad = rows(place, bt, pat, prob, grad_score, kva, kvb, query_rows.shape)
    from_x = lax.all_to_all(both, "x", 0, 0, tiled=True)
    over_x = jnp.sum(from_x.astype(f32), axis=0)
    from_y = lax.ppermute(over_x[n // 2:].astype(bf), "yh", SWAP)
    total = (over_x[: n // 2] + from_y.astype(f32)).astype(bf)
    return attended, query_grad, total[: n // 4], total[n // 4:]


def solution(mesh):
    dp, head = mesh.shape["dp"], mesh.shape["head"]
    fine = Mesh(mesh.devices.reshape(dp, head, NX, NY, NC), ("dp", "head", "x", "yh", "core"))
    spec = P(("dp", "x", "yh", "core"), "head")
    return jax.shard_map(
        per_device,
        mesh=fine,
        in_specs=(spec, spec, spec, spec, P("dp", None), P("dp", None)),
        out_specs=(spec, spec, spec, spec),
        check_vma=False,
    )
```

```python
import math

import jax
import jax.numpy as jnp
from jax import lax
from jax.experimental import pallas as pl
from jax.experimental.pallas import tpu as pltpu
from jax.sharding import Mesh, PartitionSpec as P

D = 128
BLK = 128
NX, NY, NC = 4, 2, 2
NEG = -1e30
RC = 16
VMEM_PARTS = 28
VMEM_ROWS = 16
SWAP = [(0, 1), (1, 0)]


def fill_tables(place, bt, pat, inv, tab):
    per, devs = bt.shape
    nslot = pat.shape[0]
    ns = per * nslot
    ctx, my_y, my_core = (place[i] for i in range(3))
    for dev in range(devs):
        for sub in range(per):
            inv[bt[sub, dev]] = dev * per + sub
    for b in range(per):
        seq = bt[b, ctx]
        keys = [pat[j, seq] for j in range(nslot)]
        for j in range(nslot):
            dead = jnp.int32(0)
            for i in range(j):
                dead = dead | (keys[i] == keys[j]).astype(jnp.int32)
            store = inv[keys[j]]
            sub = store & 1
            core = (store >> 1) & 1
            yh = (store >> 2) & 1
            xi = store >> 3
            away = yh ^ my_y
            t = b * nslot + j
            tab[t] = core ^ my_core
            tab[ns + t] = xi * 1024 + yh * 512 + sub * BLK
            tab[2 * ns + t] = (1 - dead) * (1 + (keys[j] == seq).astype(jnp.int32))
            tab[3 * ns + t] = xi * 1024 + away * 512 + sub * BLK


def load_keys(b, nslot, ns, tab, kva_ref, kvb_ref, kg, vg):
    for j in range(nslot):
        t = b * nslot + j
        half = tab[t]
        row = pl.multiple_of(tab[ns + t], BLK)
        dst = pl.ds(j * BLK, BLK)

        @pl.when(half == 0)
        def _():
            kg[dst, :] = kva_ref[pl.ds(row, BLK), :]
            vg[dst, :] = kva_ref[pl.ds(row + 256, BLK), :]

        @pl.when(half == 1)
        def _():
            kg[dst, :] = kvb_ref[pl.ds(row, BLK), :]
            vg[dst, :] = kvb_ref[pl.ds(row + 256, BLK), :]


def part_kernel(
    place, bt, pat, q_ref, g_ref, kva_ref, kvb_ref, pa_ref, pb_ref, p_ref, ds_ref,
    kg, vg, bias, qs, gs, s_sc, gp_sc, p_sc, ds_sc, acc_a, acc_b, inv, tab,
):
    nslot = kg.shape[0] // BLK
    per = q_ref.shape[0] // BLK
    ns = per * nslot
    heads = q_ref.shape[1] // D
    stacked = heads * BLK
    scale = D ** -0.5
    c2 = scale * math.log2(math.e)
    nt = (((1,), (1,)), ((), ()))
    tn = (((0,), (0,)), ((), ()))
    fill_tables(place, bt, pat, inv, tab)
    acc_a[...] = jnp.zeros_like(acc_a)
    acc_b[...] = jnp.zeros_like(acc_b)

    def one_block(b, _):
        r0 = pl.multiple_of(b * BLK, BLK)
        s0 = pl.multiple_of(b * stacked, stacked)
        load_keys(b, nslot, ns, tab, kva_ref, kvb_ref, kg, vg)
        for j in range(nslot):
            kind = tab[2 * ns + b * nslot + j]
            ri = lax.broadcasted_iota(jnp.int32, (BLK, BLK), 0)
            ci = lax.broadcasted_iota(jnp.int32, (BLK, BLK), 1)
            ok = jnp.logical_or(ci <= ri, kind != 2)
            ok = jnp.logical_and(ok, kind > 0)
            bias[:, j * BLK:(j + 1) * BLK] = jnp.where(ok, 0.0, NEG)
        for h in range(heads):
            qs[h * BLK:(h + 1) * BLK, :] = q_ref[pl.ds(r0, BLK), h * D:(h + 1) * D]
            gs[h * BLK:(h + 1) * BLK, :] = g_ref[pl.ds(r0, BLK), h * D:(h + 1) * D]
        s_sc[...] = lax.dot_general(qs[...], kg[...], nt, preferred_element_type=jnp.float32)
        gp_sc[...] = lax.dot_general(gs[...], vg[...], nt, preferred_element_type=jnp.float32)
        for r in range(0, stacked, RC):
            rr = slice(r, r + RC)
            out = pl.ds(s0 + r, RC)
            s = s_sc[rr, :] * c2 + bias[r % BLK:r % BLK + RC, :]
            m = jnp.max(s, axis=1, keepdims=True)
            e = jnp.exp2(s - m)
            prob = e * (1.0 / jnp.sum(e, axis=1, keepdims=True))
            p_sc[rr, :] = prob.astype(jnp.bfloat16)
            gp = gp_sc[rr, :]
            rd = jnp.sum(prob * gp, axis=1, keepdims=True)
            ds_sc[rr, :] = (prob * (gp - rd)).astype(jnp.bfloat16)
        mine = pl.ds(s0, stacked)
        p_ref[mine, :] = p_sc[...]
        ds_ref[mine, :] = ds_sc[...]
        dk_all = lax.dot_general(qs[...], ds_sc[...], tn, preferred_element_type=jnp.float32).T * scale
        dv_all = lax.dot_general(gs[...], p_sc[...], tn, preferred_element_type=jnp.float32).T
        for j in range(nslot):
            t = b * nslot + j
            half = tab[t]
            row = pl.multiple_of(tab[3 * ns + t], BLK)
            rows_k = pl.ds(row, BLK)
            rows_v = pl.ds(row + 256, BLK)
            dk_j = dk_all[j * BLK:(j + 1) * BLK]
            dv_j = dv_all[j * BLK:(j + 1) * BLK]

            @pl.when(half == 0)
            def _():
                acc_a[rows_k, :] += dk_j
                acc_a[rows_v, :] += dv_j

            @pl.when(half == 1)
            def _():
                acc_b[rows_k, :] += dk_j
                acc_b[rows_v, :] += dv_j
        return 0

    lax.fori_loop(0, per, one_block, 0)
    pa_ref[...] = acc_a[...].astype(jnp.bfloat16)
    pb_ref[...] = acc_b[...].astype(jnp.bfloat16)


def row_kernel(place, bt, pat, p_ref, ds_ref, kva_ref, kvb_ref, att_ref, qg_ref, kg, vg, inv, tab):
    nslot = kg.shape[0] // BLK
    per = att_ref.shape[0] // BLK
    heads = att_ref.shape[1] // D
    stacked = heads * BLK
    scale = D ** -0.5

    fill_tables(place, bt, pat, inv, tab)

    def one_block(b, _):
        load_keys(b, nslot, per * nslot, tab, kva_ref, kvb_ref, kg, vg)
        r0 = pl.multiple_of(b * BLK, BLK)
        mine = pl.ds(pl.multiple_of(b * stacked, stacked), stacked)
        wide = jnp.dot(p_ref[mine, :], vg[...], preferred_element_type=jnp.float32)
        qg = jnp.dot(ds_ref[mine, :], kg[...], preferred_element_type=jnp.float32) * scale
        for h in range(heads):
            cols = slice(h * D, (h + 1) * D)
            hr = slice(h * BLK, (h + 1) * BLK)
            att_ref[pl.ds(r0, BLK), cols] = wide[hr].astype(jnp.bfloat16)
            qg_ref[pl.ds(r0, BLK), cols] = qg[hr].astype(jnp.bfloat16)
        return 0

    lax.fori_loop(0, per, one_block, 0)


VM = pl.BlockSpec(memory_space=pltpu.VMEM)
SM = pl.BlockSpec(memory_space=pltpu.SMEM)


def parts(place, bt, pat, q, g, kva, kvb):
    nslot = pat.shape[0]
    per = q.shape[0] // BLK
    stacked = q.shape[1] // D * BLK
    bf, f32 = jnp.bfloat16, jnp.float32
    keys = nslot * BLK
    shapes = (kva.shape, kvb.shape, (per * stacked, keys), (per * stacked, keys))
    work = per * stacked * keys
    return pl.pallas_call(
        part_kernel,
        out_shape=tuple(jax.ShapeDtypeStruct(s, bf) for s in shapes),
        in_specs=[SM] * 3 + [VM] * 4,
        out_specs=(VM, VM, VM, VM),
        scratch_shapes=[
            pltpu.VMEM((keys, D), bf),
            pltpu.VMEM((keys, D), bf),
            pltpu.VMEM((BLK, keys), f32),
            pltpu.VMEM((stacked, D), bf),
            pltpu.VMEM((stacked, D), bf),
            pltpu.VMEM((stacked, keys), f32),
            pltpu.VMEM((stacked, keys), f32),
            pltpu.VMEM((stacked, keys), bf),
            pltpu.VMEM((stacked, keys), bf),
            pltpu.VMEM(kva.shape, f32),
            pltpu.VMEM(kvb.shape, f32),
            pltpu.SMEM((bt.shape[0] * bt.shape[1],), jnp.int32),
            pltpu.SMEM((4 * per * nslot,), jnp.int32),
        ],
        compiler_params=pltpu.CompilerParams(vmem_limit_bytes=VMEM_PARTS << 20),
        cost_estimate=pl.CostEstimate(
            flops=8 * D * work, transcendentals=work, bytes_accessed=6 << 20
        ),
        name="parts",
    )(place, bt, pat, q, g, kva, kvb)


def rows(place, bt, pat, p, ds, kva, kvb, shape):
    nslot = pat.shape[0]
    bf = jnp.bfloat16
    keys = nslot * BLK
    return pl.pallas_call(
        row_kernel,
        out_shape=tuple(jax.ShapeDtypeStruct(shape, bf) for _ in range(2)),
        in_specs=[SM] * 3 + [VM] * 4,
        out_specs=(VM, VM),
        scratch_shapes=[
            pltpu.VMEM((keys, D), bf),
            pltpu.VMEM((keys, D), bf),
            pltpu.SMEM((bt.shape[0] * bt.shape[1],), jnp.int32),
            pltpu.SMEM((4 * bt.shape[0] * nslot,), jnp.int32),
        ],
        compiler_params=pltpu.CompilerParams(vmem_limit_bytes=VMEM_ROWS << 20),
        cost_estimate=pl.CostEstimate(
            flops=4 * D * p.shape[0] * keys, transcendentals=0, bytes_accessed=6 << 20
        ),
        name="rows",
    )(place, bt, pat, p, ds, kva, kvb)


def per_device(query_rows, key_rows, value_rows, out_grad, block_table, pattern):
    my_x = lax.axis_index("x")
    my_y = lax.axis_index("yh")
    my_core = lax.axis_index("core")
    ctx = my_x * (NY * NC) + my_y * NC + my_core
    f32 = jnp.float32
    bf = jnp.bfloat16
    own = jnp.concatenate([key_rows, value_rows], axis=0)
    pair = lax.all_gather(own, "yh", axis=0, tiled=True)
    n = pair.shape[0]
    kva = lax.all_to_all(
        jnp.broadcast_to(pair[None], (NX, n, D)), "x", 0, 0, tiled=True
    ).reshape(NX * n, D)
    kvb = lax.ppermute(kva, "core", SWAP)
    place = jnp.stack([ctx, my_y, my_core]).astype(jnp.int32)
    bt, pat = block_table.T, pattern.T
    part_a, part_b, prob, grad_score = parts(place, bt, pat, query_rows, out_grad, kva, kvb)
    other = lax.ppermute(part_b, "core", SWAP)
    both = (part_a.astype(f32) + other.astype(f32)).astype(bf).reshape(NX, n, D)
    both, prob, grad_score = lax.optimization_barrier((both, prob, grad_score))
    attended, query_grad = rows(place, bt, pat, prob, grad_score, kva, kvb, query_rows.shape)
    from_x = lax.all_to_all(both, "x", 0, 0, tiled=True)
    over_x = jnp.sum(from_x.astype(f32), axis=0)
    from_y = lax.ppermute(over_x[n // 2:].astype(bf), "yh", SWAP)
    total = (over_x[: n // 2] + from_y.astype(f32)).astype(bf)
    return attended, query_grad, total[: n // 4], total[n // 4:]


def solution(mesh):
    dp, head = mesh.shape["dp"], mesh.shape["head"]
    fine = Mesh(mesh.devices.reshape(dp, head, NX, NY, NC), ("dp", "head", "x", "yh", "core"))
    spec = P(("dp", "x", "yh", "core"), "head")
    return jax.shard_map(
        per_device,
        mesh=fine,
        in_specs=(spec, spec, spec, spec, P("dp", None), P("dp", None)),
        out_specs=(spec, spec, spec, spec),
        check_vma=False,
    )
```

```python
import math

import jax
import jax.numpy as jnp
from jax import lax
from jax.experimental import pallas as pl
from jax.experimental.pallas import tpu as pltpu
from jax.sharding import Mesh, PartitionSpec as P

D = 128
BLK = 128
NX, NY, NC = 4, 2, 2
NEG = -1e30
RC = 16
VMEM_PARTS = 28
VMEM_ROWS = 16
SWAP = [(0, 1), (1, 0)]


def fill_tables(place, bt, pat, inv, tab, sums):
    per, devs = bt.shape
    nslot = pat.shape[0]
    ns = per * nslot
    ctx, my_y, my_core = (place[i] for i in range(3))
    for dev in range(devs):
        for sub in range(per):
            inv[bt[sub, dev]] = dev * per + sub
    for b in range(per):
        seq = bt[b, ctx]
        keys = [pat[j, seq] for j in range(nslot)]
        seen = jnp.int32(0)
        for j in range(nslot):
            dead = lax.shift_right_logical(seen, keys[j]) & 1
            seen = seen | lax.shift_left(jnp.int32(1), keys[j])
            store = inv[keys[j]]
            sub = store & 1
            core = (store >> 1) & 1
            yh = (store >> 2) & 1
            xi = store >> 3
            away = yh ^ my_y
            t = b * nslot + j
            tab[t] = core ^ my_core
            tab[ns + t] = xi * 1024 + yh * 512 + sub * BLK
            if not sums:
                continue
            tab[2 * ns + t] = (1 - dead) * (1 + (keys[j] == seq).astype(jnp.int32))
            tab[3 * ns + t] = xi * 1024 + away * 512 + sub * BLK


def load_keys(b, nslot, ns, tab, kva_ref, kvb_ref, kg, vg):
    for j in range(nslot):
        t = b * nslot + j
        half = tab[t]
        row = pl.multiple_of(tab[ns + t], BLK)
        dst = pl.ds(j * BLK, BLK)

        @pl.when(half == 0)
        def _():
            kg[dst, :] = kva_ref[pl.ds(row, BLK), :]
            vg[dst, :] = kva_ref[pl.ds(row + 256, BLK), :]

        @pl.when(half == 1)
        def _():
            kg[dst, :] = kvb_ref[pl.ds(row, BLK), :]
            vg[dst, :] = kvb_ref[pl.ds(row + 256, BLK), :]


def part_kernel(
    place, bt, pat, q_ref, g_ref, kva_ref, kvb_ref, pa_ref, pb_ref, p_ref, ds_ref,
    kg, vg, bias, qs, gs, s_sc, gp_sc, p_sc, ds_sc, acc_a, acc_b, inv, tab,
):
    nslot = kg.shape[0] // BLK
    per = q_ref.shape[0] // BLK
    ns = per * nslot
    heads = q_ref.shape[1] // D
    stacked = heads * BLK
    scale = D ** -0.5
    c2 = scale * math.log2(math.e)
    nt = (((1,), (1,)), ((), ()))
    tn = (((0,), (0,)), ((), ()))
    fill_tables(place, bt, pat, inv, tab, True)
    acc_a[...] = jnp.zeros_like(acc_a)
    acc_b[...] = jnp.zeros_like(acc_b)

    def one_block(b, _):
        r0 = pl.multiple_of(b * BLK, BLK)
        s0 = pl.multiple_of(b * stacked, stacked)
        load_keys(b, nslot, ns, tab, kva_ref, kvb_ref, kg, vg)
        for j in range(nslot):
            kind = tab[2 * ns + b * nslot + j]
            ri = lax.broadcasted_iota(jnp.int32, (BLK, BLK), 0)
            ci = lax.broadcasted_iota(jnp.int32, (BLK, BLK), 1)
            ok = jnp.logical_or(ci <= ri, kind != 2)
            ok = jnp.logical_and(ok, kind > 0)
            bias[:, j * BLK:(j + 1) * BLK] = jnp.where(ok, 0.0, NEG)
        for h in range(heads):
            qs[h * BLK:(h + 1) * BLK, :] = q_ref[pl.ds(r0, BLK), h * D:(h + 1) * D]
            gs[h * BLK:(h + 1) * BLK, :] = g_ref[pl.ds(r0, BLK), h * D:(h + 1) * D]
        s_sc[...] = lax.dot_general(qs[...], kg[...], nt, preferred_element_type=jnp.float32)
        gp_sc[...] = lax.dot_general(gs[...], vg[...], nt, preferred_element_type=jnp.float32)
        for r in range(0, stacked, RC):
            rr = slice(r, r + RC)
            out = pl.ds(s0 + r, RC)
            s = s_sc[rr, :] * c2 + bias[r % BLK:r % BLK + RC, :]
            m = jnp.max(s, axis=1, keepdims=True)
            e = jnp.exp2(s - m)
            prob = e * (1.0 / jnp.sum(e, axis=1, keepdims=True))
            p_sc[rr, :] = prob.astype(jnp.bfloat16)
            gp = gp_sc[rr, :]
            rd = jnp.sum(prob * gp, axis=1, keepdims=True)
            ds_sc[rr, :] = (prob * (gp - rd)).astype(jnp.bfloat16)
        mine = pl.ds(s0, stacked)
        p_ref[mine, :] = p_sc[...]
        ds_ref[mine, :] = ds_sc[...]
        dk_all = lax.dot_general(qs[...], ds_sc[...], tn, preferred_element_type=jnp.float32).T * scale
        dv_all = lax.dot_general(gs[...], p_sc[...], tn, preferred_element_type=jnp.float32).T
        for j in range(nslot):
            t = b * nslot + j
            half = tab[t]
            row = pl.multiple_of(tab[3 * ns + t], BLK)
            rows_k = pl.ds(row, BLK)
            rows_v = pl.ds(row + 256, BLK)
            dk_j = dk_all[j * BLK:(j + 1) * BLK]
            dv_j = dv_all[j * BLK:(j + 1) * BLK]

            @pl.when(half == 0)
            def _():
                acc_a[rows_k, :] += dk_j
                acc_a[rows_v, :] += dv_j

            @pl.when(half == 1)
            def _():
                acc_b[rows_k, :] += dk_j
                acc_b[rows_v, :] += dv_j
        return 0

    lax.fori_loop(0, per, one_block, 0)
    pa_ref[...] = acc_a[...].astype(jnp.bfloat16)
    pb_ref[...] = acc_b[...].astype(jnp.bfloat16)


def row_kernel(place, bt, pat, p_ref, ds_ref, kva_ref, kvb_ref, att_ref, qg_ref, kg, vg, inv, tab):
    nslot = kg.shape[0] // BLK
    per = att_ref.shape[0] // BLK
    heads = att_ref.shape[1] // D
    stacked = heads * BLK
    scale = D ** -0.5

    fill_tables(place, bt, pat, inv, tab, False)

    def one_block(b, _):
        load_keys(b, nslot, per * nslot, tab, kva_ref, kvb_ref, kg, vg)
        r0 = pl.multiple_of(b * BLK, BLK)
        mine = pl.ds(pl.multiple_of(b * stacked, stacked), stacked)
        wide = jnp.dot(p_ref[mine, :], vg[...], preferred_element_type=jnp.float32)
        qg = jnp.dot(ds_ref[mine, :], kg[...], preferred_element_type=jnp.float32) * scale
        for h in range(heads):
            cols = slice(h * D, (h + 1) * D)
            hr = slice(h * BLK, (h + 1) * BLK)
            att_ref[pl.ds(r0, BLK), cols] = wide[hr].astype(jnp.bfloat16)
            qg_ref[pl.ds(r0, BLK), cols] = qg[hr].astype(jnp.bfloat16)
        return 0

    lax.fori_loop(0, per, one_block, 0)


VM = pl.BlockSpec(memory_space=pltpu.VMEM)
SM = pl.BlockSpec(memory_space=pltpu.SMEM)


def parts(place, bt, pat, q, g, kva, kvb):
    nslot = pat.shape[0]
    per = q.shape[0] // BLK
    stacked = q.shape[1] // D * BLK
    bf, f32 = jnp.bfloat16, jnp.float32
    keys = nslot * BLK
    shapes = (kva.shape, kvb.shape, (per * stacked, keys), (per * stacked, keys))
    work = per * stacked * keys
    return pl.pallas_call(
        part_kernel,
        out_shape=tuple(jax.ShapeDtypeStruct(s, bf) for s in shapes),
        in_specs=[SM] * 3 + [VM] * 4,
        out_specs=(VM, VM, VM, VM),
        scratch_shapes=[
            pltpu.VMEM((keys, D), bf),
            pltpu.VMEM((keys, D), bf),
            pltpu.VMEM((BLK, keys), f32),
            pltpu.VMEM((stacked, D), bf),
            pltpu.VMEM((stacked, D), bf),
            pltpu.VMEM((stacked, keys), f32),
            pltpu.VMEM((stacked, keys), f32),
            pltpu.VMEM((stacked, keys), bf),
            pltpu.VMEM((stacked, keys), bf),
            pltpu.VMEM(kva.shape, f32),
            pltpu.VMEM(kvb.shape, f32),
            pltpu.SMEM((bt.shape[0] * bt.shape[1],), jnp.int32),
            pltpu.SMEM((4 * per * nslot,), jnp.int32),
        ],
        compiler_params=pltpu.CompilerParams(vmem_limit_bytes=VMEM_PARTS << 20),
        cost_estimate=pl.CostEstimate(
            flops=8 * D * work, transcendentals=work, bytes_accessed=6 << 20
        ),
        name="parts",
    )(place, bt, pat, q, g, kva, kvb)


def rows(place, bt, pat, p, ds, kva, kvb, shape):
    nslot = pat.shape[0]
    bf = jnp.bfloat16
    keys = nslot * BLK
    return pl.pallas_call(
        row_kernel,
        out_shape=tuple(jax.ShapeDtypeStruct(shape, bf) for _ in range(2)),
        in_specs=[SM] * 3 + [VM] * 4,
        out_specs=(VM, VM),
        scratch_shapes=[
            pltpu.VMEM((keys, D), bf),
            pltpu.VMEM((keys, D), bf),
            pltpu.SMEM((bt.shape[0] * bt.shape[1],), jnp.int32),
            pltpu.SMEM((4 * bt.shape[0] * nslot,), jnp.int32),
        ],
        compiler_params=pltpu.CompilerParams(vmem_limit_bytes=VMEM_ROWS << 20),
        cost_estimate=pl.CostEstimate(
            flops=4 * D * p.shape[0] * keys, transcendentals=0, bytes_accessed=6 << 20
        ),
        name="rows",
    )(place, bt, pat, p, ds, kva, kvb)


def per_device(query_rows, key_rows, value_rows, out_grad, block_table, pattern):
    my_x = lax.axis_index("x")
    my_y = lax.axis_index("yh")
    my_core = lax.axis_index("core")
    ctx = my_x * (NY * NC) + my_y * NC + my_core
    f32 = jnp.float32
    bf = jnp.bfloat16
    own = jnp.concatenate([key_rows, value_rows], axis=0)
    pair = lax.all_gather(own, "yh", axis=0, tiled=True)
    n = pair.shape[0]
    kva = lax.all_to_all(
        jnp.broadcast_to(pair[None], (NX, n, D)), "x", 0, 0, tiled=True
    ).reshape(NX * n, D)
    kvb = lax.ppermute(kva, "core", SWAP)
    place = jnp.stack([ctx, my_y, my_core]).astype(jnp.int32)
    bt, pat = block_table.T, pattern.T
    part_a, part_b, prob, grad_score = parts(place, bt, pat, query_rows, out_grad, kva, kvb)
    other = lax.ppermute(part_b, "core", SWAP)
    both = (part_a.astype(f32) + other.astype(f32)).astype(bf).reshape(NX, n, D)
    both, prob, grad_score = lax.optimization_barrier((both, prob, grad_score))
    attended, query_grad = rows(place, bt, pat, prob, grad_score, kva, kvb, query_rows.shape)
    from_x = lax.all_to_all(both, "x", 0, 0, tiled=True)
    over_x = jnp.sum(from_x.astype(f32), axis=0)
    from_y = lax.ppermute(over_x[n // 2:].astype(bf), "yh", SWAP)
    total = (over_x[: n // 2] + from_y.astype(f32)).astype(bf)
    return attended, query_grad, total[: n // 4], total[n // 4:]


def solution(mesh):
    dp, head = mesh.shape["dp"], mesh.shape["head"]
    fine = Mesh(mesh.devices.reshape(dp, head, NX, NY, NC), ("dp", "head", "x", "yh", "core"))
    spec = P(("dp", "x", "yh", "core"), "head")
    return jax.shard_map(
        per_device,
        mesh=fine,
        in_specs=(spec, spec, spec, spec, P("dp", None), P("dp", None)),
        out_specs=(spec, spec, spec, spec),
        check_vma=False,
    )
```

```python
import math

import jax
import jax.numpy as jnp
from jax import lax
from jax.experimental import pallas as pl
from jax.experimental.pallas import tpu as pltpu
from jax.sharding import Mesh, PartitionSpec as P

D = 128
BLK = 128
NX, NY, NC = 4, 2, 2
NEG = -1e30
RC = 16
VMEM_PARTS = 28
VMEM_ROWS = 16
SWAP = [(0, 1), (1, 0)]


def fill_tables(place, bt, pat, inv, tab, sums):
    per, devs = bt.shape
    nslot = pat.shape[0]
    ns = per * nslot
    ctx, my_y, my_core = (place[i] for i in range(3))
    for dev in range(devs):
        for sub in range(per):
            inv[bt[sub, dev]] = dev * per + sub
    for b in range(per):
        seq = bt[b, ctx]
        keys = [pat[j, seq] for j in range(nslot)]
        seen = jnp.int32(0)
        for j in range(nslot):
            dead = lax.shift_right_logical(seen, keys[j]) & 1
            seen = seen | lax.shift_left(jnp.int32(1), keys[j])
            store = inv[keys[j]]
            sub = store & 1
            core = (store >> 1) & 1
            yh = (store >> 2) & 1
            xi = store >> 3
            away = yh ^ my_y
            t = b * nslot + j
            tab[t] = core ^ my_core
            tab[ns + t] = xi * 1024 + yh * 512 + sub * BLK
            if not sums:
                continue
            tab[2 * ns + t] = (1 - dead) * (1 + (keys[j] == seq).astype(jnp.int32))
            tab[3 * ns + t] = xi * 1024 + away * 512 + sub * BLK


def load_keys(b, nslot, ns, tab, kva_ref, kvb_ref, kg, vg):
    for j in range(nslot):
        t = b * nslot + j
        half = tab[t]
        row = pl.multiple_of(tab[ns + t], BLK)
        dst = pl.ds(j * BLK, BLK)

        @pl.when(half == 0)
        def _():
            kg[dst, :] = kva_ref[pl.ds(row, BLK), :]
            vg[dst, :] = kva_ref[pl.ds(row + 256, BLK), :]

        @pl.when(half == 1)
        def _():
            kg[dst, :] = kvb_ref[pl.ds(row, BLK), :]
            vg[dst, :] = kvb_ref[pl.ds(row + 256, BLK), :]


def part_kernel(
    place, bt, pat, q_ref, g_ref, kva_ref, kvb_ref, pa_ref, pb_ref, p_ref, ds_ref,
    kg, vg, bias, qs, gs, s_sc, gp_sc, p_sc, ds_sc, acc_a, acc_b, inv, tab,
):
    nslot = kg.shape[0] // BLK
    per = q_ref.shape[0] // BLK
    ns = per * nslot
    heads = q_ref.shape[1] // D
    stacked = heads * BLK
    scale = D ** -0.5
    c2 = scale * math.log2(math.e)
    nt = (((1,), (1,)), ((), ()))
    tn = (((0,), (0,)), ((), ()))
    fill_tables(place, bt, pat, inv, tab, True)
    acc_a[...] = jnp.zeros_like(acc_a)
    acc_b[...] = jnp.zeros_like(acc_b)

    def one_block(b, _):
        r0 = pl.multiple_of(b * BLK, BLK)
        s0 = pl.multiple_of(b * stacked, stacked)
        load_keys(b, nslot, ns, tab, kva_ref, kvb_ref, kg, vg)
        for j in range(nslot):
            kind = tab[2 * ns + b * nslot + j]
            ri = lax.broadcasted_iota(jnp.int32, (BLK, BLK), 0)
            ci = lax.broadcasted_iota(jnp.int32, (BLK, BLK), 1)
            ok = jnp.logical_or(ci <= ri, kind != 2)
            ok = jnp.logical_and(ok, kind > 0)
            bias[:, j * BLK:(j + 1) * BLK] = jnp.where(ok, 0.0, NEG)
        for h in range(heads):
            qs[h * BLK:(h + 1) * BLK, :] = q_ref[pl.ds(r0, BLK), h * D:(h + 1) * D]
            gs[h * BLK:(h + 1) * BLK, :] = g_ref[pl.ds(r0, BLK), h * D:(h + 1) * D]
        s_sc[...] = lax.dot_general(qs[...], kg[...], nt, preferred_element_type=jnp.float32)
        gp_sc[...] = lax.dot_general(gs[...], vg[...], nt, preferred_element_type=jnp.float32)
        for r in range(0, stacked, RC):
            rr = slice(r, r + RC)
            out = pl.ds(s0 + r, RC)
            s = s_sc[rr, :] * c2 + bias[r % BLK:r % BLK + RC, :]
            m = jnp.max(s, axis=1, keepdims=True)
            e = jnp.exp2(s - m)
            prob = e * (1.0 / jnp.sum(e, axis=1, keepdims=True))
            p_sc[rr, :] = prob.astype(jnp.bfloat16)
            gp = gp_sc[rr, :]
            rd = jnp.sum(prob * gp, axis=1, keepdims=True)
            ds_sc[rr, :] = (prob * (gp - rd)).astype(jnp.bfloat16)
        mine = pl.ds(s0, stacked)
        p_ref[mine, :] = p_sc[...]
        ds_ref[mine, :] = ds_sc[...]
        dk_all = lax.dot_general(qs[...], ds_sc[...], tn, preferred_element_type=jnp.float32).T * scale
        dv_all = lax.dot_general(gs[...], p_sc[...], tn, preferred_element_type=jnp.float32).T
        for j in range(nslot):
            t = b * nslot + j
            half = tab[t]
            row = pl.multiple_of(tab[3 * ns + t], BLK)
            rows_k = pl.ds(row, BLK)
            rows_v = pl.ds(row + 256, BLK)
            dk_j = dk_all[j * BLK:(j + 1) * BLK]
            dv_j = dv_all[j * BLK:(j + 1) * BLK]

            @pl.when(half == 0)
            def _():
                acc_a[rows_k, :] += dk_j
                acc_a[rows_v, :] += dv_j

            @pl.when(half == 1)
            def _():
                acc_b[rows_k, :] += dk_j
                acc_b[rows_v, :] += dv_j
        return 0

    lax.fori_loop(0, per, one_block, 0)
    pa_ref[...] = acc_a[...].astype(jnp.bfloat16)
    pb_ref[...] = acc_b[...].astype(jnp.bfloat16)


def row_kernel(place, bt, pat, p_ref, ds_ref, kva_ref, kvb_ref, att_ref, qg_ref, kg, vg, inv, tab):
    nslot = kg.shape[0] // BLK
    per = att_ref.shape[0] // BLK
    heads = att_ref.shape[1] // D
    stacked = heads * BLK
    scale = D ** -0.5

    fill_tables(place, bt, pat, inv, tab, False)

    def one_block(b, _):
        load_keys(b, nslot, per * nslot, tab, kva_ref, kvb_ref, kg, vg)
        r0 = pl.multiple_of(b * BLK, BLK)
        mine = pl.ds(pl.multiple_of(b * stacked, stacked), stacked)
        wide = jnp.dot(p_ref[mine, :], vg[...], preferred_element_type=jnp.float32)
        qg = jnp.dot(ds_ref[mine, :], kg[...], preferred_element_type=jnp.float32) * scale
        for h in range(heads):
            cols = slice(h * D, (h + 1) * D)
            hr = slice(h * BLK, (h + 1) * BLK)
            att_ref[pl.ds(r0, BLK), cols] = wide[hr].astype(jnp.bfloat16)
            qg_ref[pl.ds(r0, BLK), cols] = qg[hr].astype(jnp.bfloat16)
        return 0

    lax.fori_loop(0, per, one_block, 0)


VM = pl.BlockSpec(memory_space=pltpu.VMEM)
SM = pl.BlockSpec(memory_space=pltpu.SMEM)


def parts(place, bt, pat, q, g, kva, kvb):
    nslot = pat.shape[0]
    per = q.shape[0] // BLK
    stacked = q.shape[1] // D * BLK
    bf, f32 = jnp.bfloat16, jnp.float32
    keys = nslot * BLK
    shapes = (kva.shape, kvb.shape, (per * stacked, keys), (per * stacked, keys))
    work = per * stacked * keys
    return pl.pallas_call(
        part_kernel,
        out_shape=tuple(jax.ShapeDtypeStruct(s, bf) for s in shapes),
        in_specs=[SM] * 3 + [VM] * 4,
        out_specs=(VM, VM, VM, VM),
        scratch_shapes=[
            pltpu.VMEM((keys, D), bf),
            pltpu.VMEM((keys, D), bf),
            pltpu.VMEM((BLK, keys), f32),
            pltpu.VMEM((stacked, D), bf),
            pltpu.VMEM((stacked, D), bf),
            pltpu.VMEM((stacked, keys), f32),
            pltpu.VMEM((stacked, keys), f32),
            pltpu.VMEM((stacked, keys), bf),
            pltpu.VMEM((stacked, keys), bf),
            pltpu.VMEM(kva.shape, f32),
            pltpu.VMEM(kvb.shape, f32),
            pltpu.SMEM((bt.shape[0] * bt.shape[1],), jnp.int32),
            pltpu.SMEM((4 * per * nslot,), jnp.int32),
        ],
        compiler_params=pltpu.CompilerParams(vmem_limit_bytes=VMEM_PARTS << 20),
        cost_estimate=pl.CostEstimate(
            flops=8 * D * work, transcendentals=work, bytes_accessed=6 << 20
        ),
        name="parts",
    )(place, bt, pat, q, g, kva, kvb)


def rows(place, bt, pat, p, ds, kva, kvb, shape):
    nslot = pat.shape[0]
    bf = jnp.bfloat16
    keys = nslot * BLK
    return pl.pallas_call(
        row_kernel,
        out_shape=tuple(jax.ShapeDtypeStruct(shape, bf) for _ in range(2)),
        in_specs=[SM] * 3 + [VM] * 4,
        out_specs=(VM, VM),
        scratch_shapes=[
            pltpu.VMEM((keys, D), bf),
            pltpu.VMEM((keys, D), bf),
            pltpu.SMEM((bt.shape[0] * bt.shape[1],), jnp.int32),
            pltpu.SMEM((4 * bt.shape[0] * nslot,), jnp.int32),
        ],
        compiler_params=pltpu.CompilerParams(vmem_limit_bytes=VMEM_ROWS << 20),
        cost_estimate=pl.CostEstimate(
            flops=4 * D * p.shape[0] * keys, transcendentals=0, bytes_accessed=6 << 20
        ),
        name="rows",
    )(place, bt, pat, p, ds, kva, kvb)


def per_device(query_rows, key_rows, value_rows, out_grad, block_table, pattern):
    my_x = lax.axis_index("x")
    my_y = lax.axis_index("yh")
    my_core = lax.axis_index("core")
    ctx = my_x * (NY * NC) + my_y * NC + my_core
    f32 = jnp.float32
    bf = jnp.bfloat16
    own = jnp.concatenate([key_rows, value_rows], axis=0)
    pair = lax.all_gather(own, "yh", axis=0, tiled=True)
    n = pair.shape[0]
    kva = lax.all_to_all(
        jnp.broadcast_to(pair[None], (NX, n, D)), "x", 0, 0, tiled=True
    ).reshape(NX * n, D)
    kvb = lax.ppermute(kva, "core", SWAP)
    place = jnp.stack([ctx, my_y, my_core]).astype(jnp.int32)
    bt, pat = block_table.T, pattern.T
    part_a, part_b, prob, grad_score = parts(place, bt, pat, query_rows, out_grad, kva, kvb)
    other = lax.ppermute(part_b, "core", SWAP)
    both = (part_a.astype(f32) + other.astype(f32)).astype(bf).reshape(NX, n, D)
    both, prob, grad_score = lax.optimization_barrier((both, prob, grad_score))
    attended, query_grad = rows(place, bt, pat, prob, grad_score, kva, kvb, query_rows.shape)
    from_x = lax.all_to_all(both, "x", 0, 0, tiled=True)
    over_x = jnp.sum(from_x.astype(f32), axis=0)
    from_y = lax.ppermute(over_x[n // 2:].astype(bf), "yh", SWAP)
    q = n // 4
    key_grad = (over_x[:q] + from_y[:q].astype(f32)).astype(bf)
    value_grad = (over_x[q:2 * q] + from_y[q:].astype(f32)).astype(bf)
    return attended, query_grad, key_grad, value_grad


def solution(mesh):
    dp, head = mesh.shape["dp"], mesh.shape["head"]
    fine = Mesh(mesh.devices.reshape(dp, head, NX, NY, NC), ("dp", "head", "x", "yh", "core"))
    spec = P(("dp", "x", "yh", "core"), "head")
    return jax.shard_map(
        per_device,
        mesh=fine,
        in_specs=(spec, spec, spec, spec, P("dp", None), P("dp", None)),
        out_specs=(spec, spec, spec, spec),
        check_vma=False,
    )
```
